32 devices in a mesh: row: 4 (over x, core), col: 2 (over y), reg: 4 (over z).
Axes of the slice: x: 2, y: 2, z: 4, core: 2. Of those that a mesh axis runs over, the one named last changes fastest.
Arguments:
- activity: bfloat16 [24576, 2048], P(('row', 'col', 'reg')), may hold values from -6 to 6
- basis: bfloat16 [24576, 64], P(('row', 'col', 'reg')), may hold values from -0.21875 to 0.21875
- region_of: int32 [192], P(('row', 'col', 'reg')), may hold values from 0 to 3
- pairs: int32 [1024, 2], P(('row', 'col', 'reg')), may hold values from 0 to 15, as said below
- lags: int32 [8], replicated, may hold values from 0 to 7, each once
Outputs:
- covariance: bfloat16 [1024, 64, 512], P(('row', 'col', 'reg'))
The draws below stay inside these ranges and needn't reach their ends.
Inputs may be any that keep to these rules, and one draw needn't show every extreme that they name: pairs[p, 0] is below 8 and pairs[p, 1] below 16.
All inputs are finite; a program needn't handle non-finite values.
Results may differ from the reference program's by a relative error of at most 0.0055.
Values may be sent and summed in bfloat16 or wider, within the bound.
A program may use at most 128 MiB of HBM per device.

```python
import jax
import jax.numpy as jnp
from jax import lax

K = 64
BLK = 128
NLAG = 8
NDEV = 768
TB = 2048
PAIR_DEV = 32
NEURONS = 24576
NBLK = 192
NPAIRS = 1024
CELLREG = 4
LEFTS = 8
RIGHTS = 16
N_ROW = 4
N_COL = 2
N_REG = 4


def draw_pairs(key, part):
    first = jax.random.fold_in(key, 11)
    second = jax.random.fold_in(key, 23)
    left = jax.random.randint(first, (NPAIRS, 1), 0, LEFTS, dtype=jnp.int32)
    right = jax.random.randint(second, (NPAIRS, 1), 0, RIGHTS, dtype=jnp.int32)
    return jnp.concatenate([left, right], axis=1)


def plant(result, stream_key, least, top_value):
    index_at = [jax.random.randint(jax.random.fold_in(stream_key, axis), (), 0, length) for axis, length in enumerate(result.shape)]
    widest = result.shape.index(max(result.shape))
    beside = index_at[:widest] + [(index_at[widest] + 1) % result.shape[widest]] + index_at[widest + 1:]
    return result.at[tuple(index_at)].set(least).at[tuple(beside)].set(top_value)


def shard_levels(key, extent, cuts, low, high):
    def one(axis_at, parts):
        draws = jax.random.uniform(jax.random.fold_in(jax.random.fold_in(key, 6), axis_at), (parts,), jnp.float32, low / len(cuts), high / len(cuts))
        return jnp.repeat(jnp.exp(draws), extent[axis_at] // parts).reshape((-1,) + (1,) * (len(extent) - axis_at - 1))

    level = one(*cuts[0])
    for cut in cuts[1:]:
        level = level * one(*cut)
    return level


def gaussian(own_key, extent, scale, limit, split=(), held_as=jnp.bfloat16):
    factor_of = shard_levels(own_key, extent, split, -0.22, 0.18) if split else 1.0
    drawn = jax.random.normal(own_key, extent, jnp.float32) * scale * factor_of
    return jnp.minimum(jnp.maximum(drawn, -limit), limit).astype(held_as)


def setup_inputs(seed: int = 0) -> dict:
    streams_of = jax.random.split(jax.random.key(seed), 6)
    activity = gaussian(streams_of[0], (NEURONS, TB), 1.0, 6.0, ((0, 32),))
    basis = gaussian(streams_of[1], (NEURONS, K), NDEV ** -0.5, 0.21875, ((0, 32),))
    region_of = plant(jax.random.randint(streams_of[2], (NBLK,), 0, CELLREG), jax.random.fold_in(streams_of[2], 1), 0, CELLREG - 1).astype(jnp.int32)
    pairs = draw_pairs(jax.random.fold_in(streams_of[5], 71), 0)
    lags = jax.random.permutation(streams_of[4], NLAG).astype(jnp.int32)
    return {"activity": activity, "basis": basis, "region_of": region_of, "pairs": pairs, "lags": lags}


def reference(activity, basis, region_of, pairs, lags):
    cells = N_ROW * N_COL
    per_cell = N_REG * NDEV // BLK
    act = activity.reshape(cells, per_cell * BLK, TB)
    bas = basis.reshape(cells, per_cell * BLK, K)
    rid = jnp.repeat(region_of.reshape(cells, per_cell), BLK, axis=1)

    def cell_signal(args):
        a, b, r = args
        match = r[:, None] == lax.iota(jnp.int32, N_REG)[None, :]
        masked = jnp.where(match[:, :, None], b[:, None, :], jnp.zeros((), jnp.bfloat16))
        masked = masked.reshape(per_cell * BLK, N_REG * K)
        return lax.dot_general(masked, a, (((0,), (0,)), ((), ())), preferred_element_type=jnp.float32)

    panel = lax.map(cell_signal, (act, bas, rid)).reshape(cells * N_REG, K, TB).astype(jnp.bfloat16)
    index = lax.iota(jnp.int32, NPAIRS)
    device = index // PAIR_DEV
    row_id = device // (N_COL * N_REG)
    col_id = (device // N_REG) % N_COL
    left = row_id * (N_COL * N_REG) + pairs[:, 0]
    right = ((pairs[:, 1] // N_REG) * N_COL + col_id) * N_REG + pairs[:, 1] % N_REG
    padded = jnp.pad(panel, ((0, 0), (0, 0), (0, NLAG)))
    scale = 1.0 / (TB ** 0.5)

    def one_pair(args):
        l, r = args
        left_panel = panel[l]
        right_panel = padded[r]
        stack = jnp.stack([lax.dynamic_slice_in_dim(right_panel, lags[m], TB, 1) for m in range(NLAG)])
        stack = stack.reshape(NLAG * K, TB)
        prod = lax.dot_general(left_panel, stack, (((1,), (1,)), ((), ())), preferred_element_type=jnp.float32)
        return (prod * scale).astype(jnp.bfloat16)

    return lax.map(one_pair, (left, right))
```

```python
import functools

import jax
import jax.numpy as jnp
from jax import lax
from jax.experimental import pallas as pl
from jax.experimental.pallas import tpu as pltpu
from jax.sharding import PartitionSpec as P

BLK = 128
TILE = 128
SPLIT = 4
HOP = 2
CROSS = 2
TURN = 2
GROUP = 4


def panels_kernel(
    shape, ntile, region_ref, pairs_ref, basis_ref, act_ref, raw_ref,
    masked, act, own, up_in, down_in, up_out, down_out, lefts, rights, lstack, rstack, acc,
    act_sem, up_send, up_recv, down_send, down_recv,
    x_send, x_recv, y_send, y_recv, sib_send, sib_recv,
):
    nrow, ncol, nreg = shape
    nx = nrow // 2
    width, neurons = basis_ref.shape
    npairs = acc.shape[0]
    bins = ntile * TILE
    i, j, g = lax.axis_index("row"), lax.axis_index("col"), lax.axis_index("reg")
    x, core = i // 2, i % 2
    sib = {"row": x * 2 + 1 - core}
    last = nreg - 1

    def x_row(k):
        return ((x + k) % nx) * 2 + core

    def col_at(k):
        return (j + k) % ncol

    def load(c):
        return pltpu.make_async_copy(
            act_ref.at[:, pl.ds(pl.multiple_of(c * TILE, TILE), TILE)], act.at[c], act_sem.at[c]
        )

    @pl.loop(0, ntile)
    def _(c):
        load(c).start()

    barrier = pltpu.get_barrier_semaphore()

    def greet(peer):
        pl.semaphore_signal(barrier, inc=1, device_id=peer, device_id_type=pl.DeviceIdType.MESH)

    @pl.when(g > 0)
    def _():
        greet({"reg": g - 1})

    @pl.when(g < last)
    def _():
        greet({"reg": g + 1})

    for k in range(1, nx):
        greet({"row": x_row(k)})
    for k in range(1, ncol):
        greet({"col": col_at(k)})
    greet(sib)

    def remote(src, dst, send_sem, recv_sem, peer):
        return pltpu.make_async_remote_copy(
            src_ref=src, dst_ref=dst, send_sem=send_sem, recv_sem=recv_sem,
            device_id=peer, device_id_type=pl.DeviceIdType.MESH,
        )

    def up(c):
        return remote(up_out.at[c], up_in.at[c], up_send.at[c], up_recv.at[c], {"reg": g + 1})

    def down(c):
        return remote(down_out.at[c], down_in.at[c], down_send.at[c], down_recv.at[c], {"reg": g - 1})

    def across_x(k, c, row):
        here = rights.at[row, c]
        return remote(here, here, x_send.at[k - 1, c], x_recv.at[k - 1, c], {"row": x_row(k)})

    def across_y(k, c, col):
        return remote(
            rights.at[i, c], lefts.at[col, c + 1], y_send.at[k - 1, c], y_recv.at[k - 1, c],
            {"col": col_at(k)},
        )

    def to_sib(k, c, row):
        here = rights.at[row, c]
        return remote(here, here, sib_send.at[k, c], sib_recv.at[k, c], sib)

    for n in range(neurons // BLK):
        block = basis_ref[:, n * BLK:(n + 1) * BLK]
        for r in range(nreg):
            masked[r * width:(r + 1) * width, n * BLK:(n + 1) * BLK] = jnp.where(
                region_ref[n] == r, block, jnp.zeros_like(block)
            )

    blank = jnp.zeros((nreg * width, TILE), jnp.bfloat16)
    for col in range(ncol):
        lefts[col, 0] = blank
    for row in range(nrow):
        rights[row, ntile] = blank

    @pl.when(g == 0)
    def _():
        @pl.loop(0, ntile)
        def _(c):
            up_in[c] = blank

    @pl.when(g == last)
    def _():
        @pl.loop(0, ntile)
        def _(c):
            down_in[c] = blank

    @pl.loop(0, npairs)
    def _(p):
        acc[p] = jnp.zeros(acc.shape[1:], jnp.float32)

    ends = jnp.where(jnp.logical_or(g == 0, g == last), 1, 2)
    pl.semaphore_wait(barrier, ends + nx + ncol - 1)

    def inside(c):
        return jnp.logical_and(c >= 0, c < ntile)

    def project(c):
        load(c).wait()
        part = jnp.dot(masked[...], act[c], preferred_element_type=jnp.float32)
        own[c] = part

        @pl.when(g == 0)
        def _():
            up_out[c] = part.astype(jnp.bfloat16)
            up(c).start()

        @pl.when(g == last)
        def _():
            down_out[c] = part.astype(jnp.bfloat16)
            down(c).start()

    def climb(c):
        up(c).wait_recv()

        @pl.when(g < last)
        def _():
            up_out[c] = (own[c] + up_in[c].astype(jnp.float32)).astype(jnp.bfloat16)
            up(c).start()

    def descend(c):
        down(c).wait_recv()

        @pl.when(g > 0)
        def _():
            down_out[c] = (own[c] + down_in[c].astype(jnp.float32)).astype(jnp.bfloat16)
            down(c).start()

    def total(c):
        panel = own[c] + up_in[c].astype(jnp.float32) + down_in[c].astype(jnp.float32)
        panel = panel.astype(jnp.bfloat16)
        rights[i, c] = panel
        lefts[j, c + 1] = panel
        for k in range(1, nx):
            across_x(k, c, i).start()
        for k in range(1, ncol):
            across_y(k, c, j).start()
        to_sib(0, c, i).start()

    def pass_on(c):
        for k in range(1, nx):
            row = ((x - k + nx) % nx) * 2 + core
            across_x(k, c, row).wait_recv()
            to_sib(k, c, row).start()

    def landed(c):
        for k in range(1, ncol):
            across_y(k, c, (j - k + ncol) % ncol).wait_recv()
        to_sib(0, c, x * 2 + 1 - core).wait_recv()
        for k in range(1, nx):
            to_sib(k, c, ((x - k + nx) % nx) * 2 + 1 - core).wait_recv()

    def correlate(b):
        first = 2 * b
        for col in range(ncol):
            for r in range(nreg):
                rows = slice(r * width, (r + 1) * width)
                tiles = jnp.concatenate([lefts[col, first + t, rows, :] for t in range(3)], axis=1)
                lstack[col * nreg + r, :width, :] = tiles[:, TILE:]
                for m in range(1, SPLIT):
                    lstack[col * nreg + r, m * width:(m + 1) * width, :] = pltpu.roll(tiles, m, 1)[:, TILE:]
        for row in range(nrow):
            for r in range(nreg):
                rows = slice(r * width, (r + 1) * width)
                tiles = jnp.concatenate([rights[row, first + t, rows, :] for t in range(3)], axis=1)
                rstack[row * nreg + r, :width, :] = tiles[:, :2 * TILE]
                rstack[row * nreg + r, width:, :] = pltpu.roll(tiles, 3 * TILE - SPLIT, 1)[:, :2 * TILE]

        @pl.loop(0, npairs // GROUP)
        def _(q):
            for n in range(GROUP):
                p = q * GROUP + n
                acc[p] += lax.dot_general(
                    lstack[pairs_ref[0, p]], rstack[pairs_ref[1, p]], (((1,), (1,)), ((), ())),
                    preferred_element_type=jnp.float32,
                )

    @pl.loop(0, ntile + HOP * last + CROSS + TURN)
    def _(s):
        @pl.when(s < ntile)
        def _():
            project(s)

        @pl.when(jnp.logical_and(g > 0, inside(s - HOP * g)))
        def _():
            climb(s - HOP * g)

        @pl.when(jnp.logical_and(g < last, inside(s - HOP * (last - g))))
        def _():
            descend(s - HOP * (last - g))

        done = s - HOP * jnp.maximum(g, last - g)

        @pl.when(inside(done))
        def _():
            total(done)

        @pl.when(inside(done - CROSS))
        def _():
            pass_on(done - CROSS)

        here = done - CROSS - TURN

        @pl.when(inside(here))
        def _():
            landed(here)

        @pl.when(jnp.logical_and(inside(here), jnp.logical_and(here >= 2, here % 2 == 0)))
        def _():
            correlate(here // 2 - 1)

        @pl.when(here == ntile - 1)
        def _():
            correlate(ntile // 2 - 1)

    @pl.loop(0, npairs)
    def _(p):
        raw_ref[p] = (acc[p] * (1.0 / bins**0.5)).astype(jnp.bfloat16)

    @pl.loop(0, ntile)
    def _(c):
        @pl.when(g < last)
        def _():
            up(c).wait_send()

        @pl.when(g > 0)
        def _():
            down(c).wait_send()

        for k in range(1, nx):
            across_x(k, c, i).wait_send()
        for k in range(1, ncol):
            across_y(k, c, j).wait_send()
        for k in range(nx):
            to_sib(k, c, i).wait_send()


def raw_covariances(shape, region_of, pairs, basis, activity):
    nrow, ncol, nreg = shape
    nx = nrow // 2
    width, neurons = basis.shape
    npairs = pairs.shape[1]
    ntile = activity.shape[1] // TILE
    tall = nreg * width
    dma = pltpu.SemaphoreType.DMA
    tiles = pltpu.VMEM((ntile, tall, TILE), jnp.bfloat16)
    return pl.pallas_call(
        functools.partial(panels_kernel, shape, ntile),
        in_specs=[
            pl.BlockSpec(memory_space=pltpu.SMEM),
            pl.BlockSpec(memory_space=pltpu.SMEM),
            pl.BlockSpec(memory_space=pltpu.VMEM),
            pl.BlockSpec(memory_space=pltpu.HBM),
        ],
        out_specs=pl.BlockSpec(memory_space=pltpu.VMEM),
        out_shape=jax.ShapeDtypeStruct((npairs, SPLIT * width, 2 * width), jnp.bfloat16),
        scratch_shapes=[
            pltpu.VMEM((tall, neurons), jnp.bfloat16),
            pltpu.VMEM((ntile, neurons, TILE), jnp.bfloat16),
            pltpu.VMEM((ntile, tall, TILE), jnp.float32),
            tiles, tiles, tiles, tiles,
            pltpu.VMEM((ncol, ntile + 1, tall, TILE), jnp.bfloat16),
            pltpu.VMEM((nrow, ntile + 1, tall, TILE), jnp.bfloat16),
            pltpu.VMEM((ncol * nreg, SPLIT * width, 2 * TILE), jnp.bfloat16),
            pltpu.VMEM((nrow * nreg, 2 * width, 2 * TILE), jnp.bfloat16),
            pltpu.VMEM((npairs, SPLIT * width, 2 * width), jnp.float32),
            dma((ntile,)),
        ]
        + [dma((ntile,))] * 4
        + [dma((nx - 1, ntile))] * 2
        + [dma((ncol - 1, ntile))] * 2
        + [dma((nx, ntile))] * 2,
        compiler_params=pltpu.CompilerParams(
            collective_id=0, has_side_effects=True, vmem_limit_bytes=56 << 20
        ),
    )(region_of, pairs, basis, activity)


def order_kernel(lags_ref, raw_ref, out_ref):
    group, width, _ = out_ref.shape
    low = lax.broadcasted_iota(jnp.int32, (width, 2 * width), 1) < width
    for q in range(group):
        for s in range(lags_ref.shape[0] // 2):
            first, second = lags_ref[2 * s], lags_ref[2 * s + 1]
            a = raw_ref[q, first % SPLIT]
            b = raw_ref[q, second % SPLIT]
            a = jnp.where(first < SPLIT, a, pltpu.roll(a, width, 1))
            b = jnp.where(second < SPLIT, pltpu.roll(b, width, 1), b)
            out_ref[q, :, s * 2 * width:(s + 1) * 2 * width] = jnp.where(low, a, b)


def ordered(raw, lags):
    npairs, tall, wide = raw.shape
    width = wide // 2
    group = 8
    return pl.pallas_call(
        order_kernel,
        grid=(npairs // group,),
        in_specs=[
            pl.BlockSpec(memory_space=pltpu.SMEM),
            pl.BlockSpec((group, SPLIT, width, wide), lambda p: (p, 0, 0, 0)),
        ],
        out_specs=pl.BlockSpec((group, width, lags.shape[0] * width), lambda p: (p, 0, 0)),
        out_shape=jax.ShapeDtypeStruct((npairs, width, lags.shape[0] * width), jnp.bfloat16),
    )(lags, raw.reshape(npairs, SPLIT, width, wide))


def local(shape, activity, basis, region_of, pairs, lags):
    raw = raw_covariances(shape, region_of, pairs.T, basis.T, activity)
    return ordered(raw, lags)


def solution(mesh):
    shape = (mesh.shape["row"], mesh.shape["col"], mesh.shape["reg"])
    return jax.shard_map(
        functools.partial(local, shape),
        mesh=mesh,
        in_specs=(
            P(("row", "col", "reg"), None),
            P(("row", "col", "reg"), None),
            P(("row", "col", "reg")),
            P(("row", "col", "reg"), None),
            P(),
        ),
        out_specs=P(("row", "col", "reg"), None, None),
        check_vma=False,
    )
```

```python
import functools

import jax
import jax.numpy as jnp
from jax import lax
from jax.experimental import pallas as pl
from jax.experimental.pallas import tpu as pltpu
from jax.sharding import PartitionSpec as P

BLK = 128
PHASES = 16
RUN = 16
SPAN = PHASES * RUN
TILE = SPAN // 2
SPLIT = 4
HOP = 3
CROSS = 4
TURN = 2


def wrapped(now, beside, by):
    rows = now.shape[0]
    now, beside = now.astype(jnp.float32), beside.astype(jnp.float32)
    row = lax.broadcasted_iota(jnp.int32, now.shape, 0) % RUN
    edge = 0 if by > 0 else RUN - 1
    moved = pltpu.roll(now, by % rows, 0)
    missing = pltpu.roll(beside, (-by * (RUN - 1)) % rows, 0)
    return jnp.where(row == edge, missing, moved).astype(jnp.bfloat16)


def panels_kernel(
    shape, ntile, region_ref, pairs_ref, basis_ref, act_ref, raw_ref,
    masked, act, order, own, up_in, down_in, up_out, down_out, lefts, rights, lstack, rstack, acc,
    act_sem, up_send, up_recv, down_send, down_recv,
    x_send, x_recv, y_send, y_recv, sib_send, sib_recv,
):
    nrow, ncol, nreg = shape
    nx = nrow // 2
    width, neurons = basis_ref.shape
    npairs = acc.shape[0]
    bins = ntile * TILE
    nblock = ntile // 2
    i, j, g = lax.axis_index("row"), lax.axis_index("col"), lax.axis_index("reg")
    x, core = i // 2, i % 2
    sib = {"row": x * 2 + 1 - core}
    last = nreg - 1

    def x_row(k):
        return ((x + k) % nx) * 2 + core

    def col_at(k):
        return (j + k) % ncol

    def load(c):
        return pltpu.make_async_copy(
            act_ref.at[:, pl.ds(pl.multiple_of(c * SPAN, SPAN), SPAN)], act.at[c], act_sem.at[c]
        )

    @pl.loop(0, nblock)
    def _(c):
        load(c).start()

    barrier = pltpu.get_barrier_semaphore()

    def greet(peer):
        pl.semaphore_signal(barrier, inc=1, device_id=peer, device_id_type=pl.DeviceIdType.MESH)

    @pl.when(g > 0)
    def _():
        greet({"reg": g - 1})

    @pl.when(g < last)
    def _():
        greet({"reg": g + 1})

    for k in range(1, nx):
        greet({"row": x_row(k)})
    for k in range(1, ncol):
        greet({"col": col_at(k)})
    greet(sib)

    def remote(src, dst, send_sem, recv_sem, peer):
        return pltpu.make_async_remote_copy(
            src_ref=src, dst_ref=dst, send_sem=send_sem, recv_sem=recv_sem,
            device_id=peer, device_id_type=pl.DeviceIdType.MESH,
        )

    def up(c):
        return remote(up_out.at[c], up_in.at[c], up_send.at[c], up_recv.at[c], {"reg": g + 1})

    def down(c):
        return remote(down_out.at[c], down_in.at[c], down_send.at[c], down_recv.at[c], {"reg": g - 1})

    def across_x(k, c, row):
        here = rights.at[row, c]
        return remote(here, here, x_send.at[k - 1, c], x_recv.at[k - 1, c], {"row": x_row(k)})

    def across_y(k, c, col):
        return remote(
            rights.at[i, c], lefts.at[col, c + 1], y_send.at[k - 1, c], y_recv.at[k - 1, c],
            {"col": col_at(k)},
        )

    def to_sib(k, c, row):
        here = rights.at[row, c]
        return remote(here, here, sib_send.at[k, c], sib_recv.at[k, c], sib)

    for n in range(neurons // BLK):
        block = basis_ref[:, n * BLK:(n + 1) * BLK].T
        masked[n * BLK:(n + 1) * BLK, :] = jnp.concatenate(
            [jnp.where(region_ref[n] == r, block, jnp.zeros_like(block)) for r in range(nreg)], axis=1
        )

    blank = jnp.zeros((TILE, nreg * width), jnp.bfloat16)
    for col in range(ncol):
        lefts[col, 0] = blank
    for row in range(nrow):
        rights[row, ntile] = blank

    @pl.when(g == 0)
    def _():
        @pl.loop(0, ntile)
        def _(c):
            up_in[c] = blank

    @pl.when(g == last)
    def _():
        @pl.loop(0, ntile)
        def _(c):
            down_in[c] = blank

    @pl.loop(0, npairs)
    def _(p):
        acc[p] = jnp.zeros(acc.shape[1:], jnp.float32)

    ends = jnp.where(jnp.logical_or(g == 0, g == last), 1, 2)
    pl.semaphore_wait(barrier, ends + nx + ncol - 1)

    def inside(c):
        return jnp.logical_and(c >= 0, c < ntile)

    def project(b):
        load(b).wait()
        part = lax.dot_general(
            act[b], masked[...], (((0,), (0,)), ((), ())), preferred_element_type=jnp.float32
        )
        for q in range(nreg * width // 128):
            order[q] = part[:, q * 128:(q + 1) * 128]
        for u in range(PHASES):
            c = 2 * b + u * RUN // TILE
            first = u * RUN % TILE
            for q in range(nreg * width // 128):
                own[c, first:first + RUN, q * 128:(q + 1) * 128] = order[q, pl.ds(u, RUN, stride=PHASES), :]

        @pl.when(g == 0)
        def _():
            for c in (2 * b, 2 * b + 1):
                up_out[c] = own[c].astype(jnp.bfloat16)
                up(c).start()

        @pl.when(g == last)
        def _():
            for c in (2 * b, 2 * b + 1):
                down_out[c] = own[c].astype(jnp.bfloat16)
                down(c).start()

    def climb(c):
        up(c).wait_recv()

        @pl.when(g < last)
        def _():
            up_out[c] = (own[c] + up_in[c].astype(jnp.float32)).astype(jnp.bfloat16)
            up(c).start()

    def descend(c):
        down(c).wait_recv()

        @pl.when(g > 0)
        def _():
            down_out[c] = (own[c] + down_in[c].astype(jnp.float32)).astype(jnp.bfloat16)
            down(c).start()

    def total(c):
        panel = own[c] + up_in[c].astype(jnp.float32) + down_in[c].astype(jnp.float32)
        panel = panel.astype(jnp.bfloat16)
        rights[i, c] = panel
        lefts[j, c + 1] = panel
        for k in range(1, nx):
            across_x(k, c, i).start()
        for k in range(1, ncol):
            across_y(k, c, j).start()
        to_sib(0, c, i).start()

    def pass_on(c):
        for k in range(1, nx):
            row = ((x - k + nx) % nx) * 2 + core
            across_x(k, c, row).wait_recv()
            to_sib(k, c, row).start()

    def landed(c):
        for k in range(1, ncol):
            across_y(k, c, (j - k + ncol) % ncol).wait_recv()
        to_sib(0, c, x * 2 + 1 - core).wait_recv()
        for k in range(1, nx):
            to_sib(k, c, ((x - k + nx) % nx) * 2 + 1 - core).wait_recv()

    low = lax.broadcasted_iota(jnp.int32, (SPAN, 2 * width), 1) < width

    def correlate(b):
        @pl.loop(0, ncol)
        def _(col):
            for q in range(nreg // 2):
                lanes = slice(q * 2 * width, (q + 1) * 2 * width)
                wrap = SPLIT * RUN
                before = lefts[col, 2 * b, TILE - wrap:, lanes]
                half = [lefts[col, 2 * b + 1, :, lanes], lefts[col, 2 * b + 2, :, lanes]]
                both = jnp.concatenate([wrapped(half[1][TILE - wrap:], before, 1)] + half, axis=0)
                turned = pltpu.roll(both, width, 1)
                even = jnp.where(low, both[wrap:], turned[:SPAN])
                odd = jnp.where(low, turned[wrap:], both[:SPAN])
                lstack[col * nreg + 2 * q] = even.T
                lstack[col * nreg + 2 * q + 1] = odd.T

        @pl.loop(0, nrow)
        def _(row):
            for q in range(nreg // 2):
                lanes = slice(q * 2 * width, (q + 1) * 2 * width)
                wrap = (SPLIT - 1) * RUN
                half = [rights[row, 2 * b, :, lanes], rights[row, 2 * b + 1, :, lanes]]
                after = rights[row, 2 * b + 2, :wrap, lanes]
                both = jnp.concatenate(half + [wrapped(half[0][:wrap], after, -1)], axis=0)
                turned = pltpu.roll(both, width, 1)
                for m in range(0, SPLIT, 2):
                    now, then = slice(m * RUN, m * RUN + SPAN), slice((m + 1) * RUN, (m + 1) * RUN + SPAN)
                    out = slice(m * width, (m + 2) * width)
                    rstack[row * nreg + 2 * q, :, out] = jnp.where(low, both[now], turned[then])
                    rstack[row * nreg + 2 * q + 1, :, out] = jnp.where(low, turned[now], both[then])

        for p in range(npairs):
            acc[p] += jnp.dot(
                lstack[pairs_ref[0, p]], rstack[pairs_ref[1, p]], preferred_element_type=jnp.float32
            )

    project(0)

    @pl.loop(0, ntile + HOP * last + CROSS + TURN)
    def _(s):
        @pl.when(jnp.logical_and(g > 0, inside(s - HOP * g)))
        def _():
            climb(s - HOP * g)

        @pl.when(jnp.logical_and(g < last, inside(s - HOP * (last - g))))
        def _():
            descend(s - HOP * (last - g))

        done = s - HOP * jnp.maximum(g, last - g)

        @pl.when(inside(done))
        def _():
            total(done)

        @pl.when(inside(done - CROSS))
        def _():
            pass_on(done - CROSS)

        @pl.when(jnp.logical_and(s % 2 == 0, s // 2 + 1 < nblock))
        def _():
            project(s // 2 + 1)

        here = done - CROSS - TURN

        @pl.when(inside(here))
        def _():
            landed(here)

        final = here == ntile - 1
        even = jnp.logical_and(inside(here), jnp.logical_and(here >= 2, here % 2 == 0))

        @pl.when(jnp.logical_or(even, final))
        def _():
            correlate(jnp.where(final, nblock - 1, here // 2 - 1))

    @pl.loop(0, npairs)
    def _(p):
        done = (acc[p] * (1.0 / bins**0.5)).astype(jnp.bfloat16)
        for q in range(SPLIT // 2):
            raw_ref[p, q] = done[:, q * 2 * width:(q + 1) * 2 * width]

    @pl.loop(0, ntile)
    def _(c):
        @pl.when(g < last)
        def _():
            up(c).wait_send()

        @pl.when(g > 0)
        def _():
            down(c).wait_send()

        for k in range(1, nx):
            across_x(k, c, i).wait_send()
        for k in range(1, ncol):
            across_y(k, c, j).wait_send()
        for k in range(nx):
            to_sib(k, c, i).wait_send()


def raw_covariances(shape, region_of, pairs, basis, activity):
    nrow, ncol, nreg = shape
    nx = nrow // 2
    width, neurons = basis.shape
    npairs = pairs.shape[1]
    ntile = activity.shape[1] // TILE
    tall = nreg * width
    dma = pltpu.SemaphoreType.DMA
    tiles = pltpu.VMEM((ntile, TILE, tall), jnp.bfloat16)
    return pl.pallas_call(
        functools.partial(panels_kernel, shape, ntile),
        in_specs=[
            pl.BlockSpec(memory_space=pltpu.SMEM),
            pl.BlockSpec(memory_space=pltpu.SMEM),
            pl.BlockSpec(memory_space=pltpu.VMEM),
            pl.BlockSpec(memory_space=pltpu.HBM),
        ],
        out_specs=pl.BlockSpec(memory_space=pltpu.VMEM),
        out_shape=jax.ShapeDtypeStruct((npairs, SPLIT // 2, 2 * width, 2 * width), jnp.bfloat16),
        scratch_shapes=[
            pltpu.VMEM((neurons, tall), jnp.bfloat16),
            pltpu.VMEM((ntile // 2, neurons, SPAN), jnp.bfloat16),
            pltpu.VMEM((tall // 128, SPAN, 128), jnp.float32),
            pltpu.VMEM((ntile, TILE, tall), jnp.float32),
            tiles, tiles, tiles, tiles,
            pltpu.VMEM((ncol, ntile + 1, TILE, tall), jnp.bfloat16),
            pltpu.VMEM((nrow, ntile + 1, TILE, tall), jnp.bfloat16),
            pltpu.VMEM((ncol * nreg, 2 * width, SPAN), jnp.bfloat16),
            pltpu.VMEM((nrow * nreg, SPAN, SPLIT * width), jnp.bfloat16),
            pltpu.VMEM((npairs, 2 * width, SPLIT * width), jnp.float32),
            dma((ntile // 2,)),
        ]
        + [dma((ntile,))] * 4
        + [dma((nx - 1, ntile))] * 2
        + [dma((ncol - 1, ntile))] * 2
        + [dma((nx, ntile))] * 2,
        compiler_params=pltpu.CompilerParams(
            collective_id=0, has_side_effects=True, vmem_limit_bytes=56 << 20
        ),
    )(region_of, pairs, basis, activity)


def order_kernel(lags_ref, raw_ref, out_ref):
    group, width, _ = out_ref.shape
    low = lax.broadcasted_iota(jnp.int32, (width, 2 * width), 1) < width
    for q in range(group):
        for s in range(lags_ref.shape[0] // 2):
            first, second = lags_ref[2 * s], lags_ref[2 * s + 1]
            a = raw_ref[q, first // 2 % 2, first // SPLIT]
            b = raw_ref[q, second // 2 % 2, second // SPLIT]
            a = jnp.where(first % 2 == 0, a, pltpu.roll(a, width, 1))
            b = jnp.where(second % 2 == 0, pltpu.roll(b, width, 1), b)
            out_ref[q, :, s * 2 * width:(s + 1) * 2 * width] = jnp.where(low, a, b)


def ordered(raw, lags):
    npairs, halves, tall, wide = raw.shape
    width = wide // 2
    group = 8
    return pl.pallas_call(
        order_kernel,
        grid=(npairs // group,),
        in_specs=[
            pl.BlockSpec(memory_space=pltpu.SMEM),
            pl.BlockSpec((group, halves, 2, width, wide), lambda p: (p, 0, 0, 0, 0)),
        ],
        out_specs=pl.BlockSpec((group, width, lags.shape[0] * width), lambda p: (p, 0, 0)),
        out_shape=jax.ShapeDtypeStruct((npairs, width, lags.shape[0] * width), jnp.bfloat16),
    )(lags, raw.reshape(npairs, halves, 2, width, wide))


def local(shape, activity, basis, region_of, pairs, lags):
    raw = raw_covariances(shape, region_of, pairs.T, basis.T, activity)
    return ordered(raw, lags)


def solution(mesh):
    shape = (mesh.shape["row"], mesh.shape["col"], mesh.shape["reg"])
    return jax.shard_map(
        functools.partial(local, shape),
        mesh=mesh,
        in_specs=(
            P(("row", "col", "reg"), None),
            P(("row", "col", "reg"), None),
            P(("row", "col", "reg")),
            P(("row", "col", "reg"), None),
            P(),
        ),
        out_specs=P(("row", "col", "reg"), None, None),
        check_vma=False,
    )
```

```python
import functools

import jax
import jax.numpy as jnp
from jax import lax
from jax.experimental import pallas as pl
from jax.experimental.pallas import tpu as pltpu
from jax.sharding import PartitionSpec as P

BLK = 128
PHASES = 16
RUN = 16
SPAN = PHASES * RUN
HALF = SPAN // 2
BIG, SMALL = 64, 32
NSMALL = 4
DEPTH = 256
HOP = 3
CROSS = 4
TURN = 2


def wrapped(now, after):
    rows = now.shape[0]
    at = lax.broadcasted_iota(jnp.int32, now.shape, 0) % RUN
    moved = pltpu.roll(now.astype(jnp.float32), rows - 1, 0)
    missing = pltpu.roll(after.astype(jnp.float32), RUN - 1, 0)
    return jnp.where(at == RUN - 1, missing, moved).astype(jnp.bfloat16)


def panels_kernel(
    shape, nlag, region_ref, pairs_ref, basis_ref, act_ref, raw_ref,
    masked, act, natural, own, up_in, down_in, up_out, down_out, lefts, rights, lhs, rhs, acc, odd_acc,
    act_sem, up_send, up_recv, down_send, down_recv,
    x_send, x_recv, y_send, y_recv, sib_send, sib_recv,
):
    nrow, ncol, nreg = shape
    nx = nrow // 2
    width, neurons = basis_ref.shape
    wide = 2 * width
    npairs = acc.shape[0]
    nblock = act.shape[0]
    bins = nblock * SPAN
    total_rows = bins // 2
    nbig = (total_rows - NSMALL * SMALL) // BIG
    ntile = nbig + NSMALL
    ahead = nlag // 2 * RUN
    i, j, g = lax.axis_index("row"), lax.axis_index("col"), lax.axis_index("reg")
    x, core = i // 2, i % 2
    sib = {"row": x * 2 + 1 - core}
    last = nreg - 1

    def x_row(k):
        return ((x + k) % nx) * 2 + core

    def col_at(k):
        return (j + k) % ncol

    def load(b):
        return pltpu.make_async_copy(
            act_ref.at[:, pl.ds(pl.multiple_of(b * SPAN, SPAN), SPAN)], act.at[b], act_sem.at[b]
        )

    @pl.loop(0, nblock)
    def _(b):
        load(b).start()

    barrier = pltpu.get_barrier_semaphore()

    def greet(peer):
        pl.semaphore_signal(barrier, inc=1, device_id=peer, device_id_type=pl.DeviceIdType.MESH)

    @pl.when(g > 0)
    def _():
        greet({"reg": g - 1})

    @pl.when(g < last)
    def _():
        greet({"reg": g + 1})

    for k in range(1, nx):
        greet({"row": x_row(k)})
    for k in range(1, ncol):
        greet({"col": col_at(k)})
    greet(sib)

    def remote(src, dst, send_sem, recv_sem, peer):
        return pltpu.make_async_remote_copy(
            src_ref=src, dst_ref=dst, send_sem=send_sem, recv_sem=recv_sem,
            device_id=peer, device_id_type=pl.DeviceIdType.MESH,
        )

    def up(c, rows):
        return remote(up_out.at[rows], up_in.at[rows], up_send.at[c], up_recv.at[c], {"reg": g + 1})

    def down(c, rows):
        return remote(down_out.at[rows], down_in.at[rows], down_send.at[c], down_recv.at[c], {"reg": g - 1})

    def across_x(k, c, rows, row):
        here = rights.at[row, rows]
        return remote(here, here, x_send.at[k - 1, c], x_recv.at[k - 1, c], {"row": x_row(k)})

    def across_y(k, c, rows, col):
        return remote(
            rights.at[i, rows], lefts.at[col, rows], y_send.at[k - 1, c], y_recv.at[k - 1, c],
            {"col": col_at(k)},
        )

    def to_sib(k, c, rows, row):
        here = rights.at[row, rows]
        return remote(here, here, sib_send.at[k, c], sib_recv.at[k, c], sib)

    for n in range(neurons // BLK):
        block = basis_ref[:, n * BLK:(n + 1) * BLK].T
        masked[n * BLK:(n + 1) * BLK, :] = jnp.concatenate(
            [jnp.where(region_ref[n] == r // 2, block, jnp.zeros_like(block)) for r in range(2 * nreg)], axis=1
        )

    @pl.when(g == 0)
    def _():
        up_in[...] = jnp.zeros_like(up_in)

    @pl.when(g == last)
    def _():
        down_in[...] = jnp.zeros_like(down_in)

    low = lax.broadcasted_iota(jnp.int32, (RUN, wide), 1) < width

    def project(b):
        load(b).wait()
        part = lax.dot_general(
            act[b], masked[...], (((0,), (0,)), ((), ())), preferred_element_type=jnp.float32
        )
        for r in range(nreg):
            natural[r] = part[:, r * wide:(r + 1) * wide]
        for n in range(HALF // RUN):
            rows = pl.ds(pl.multiple_of(b * HALF + n * RUN, RUN), RUN)
            for r in range(nreg):
                own[rows, r * wide:(r + 1) * wide] = jnp.where(
                    low,
                    natural[r, pl.ds(2 * n, RUN, stride=PHASES), :],
                    natural[r, pl.ds(2 * n + 1, RUN, stride=PHASES), :],
                )

    project(0)
    ends = jnp.where(jnp.logical_or(g == 0, g == last), 1, 2)
    pl.semaphore_wait(barrier, ends + nx + ncol - 1)

    def each_size(c, act_on):
        @pl.when(jnp.logical_and(c >= 0, c < nbig))
        def _():
            first = pl.multiple_of(c * BIG, BIG)
            act_on(pl.ds(first, BIG), first, BIG)

        @pl.when(jnp.logical_and(c >= nbig, c < ntile))
        def _():
            first = pl.multiple_of(nbig * BIG + (c - nbig) * SMALL, SMALL)
            act_on(pl.ds(first, SMALL), first, SMALL)

    def begin(c):
        def act_on(rows, first, size):
            @pl.when(g == 0)
            def _():
                up_out[rows] = own[rows].astype(jnp.bfloat16)
                up(c, rows).start()

            @pl.when(g == last)
            def _():
                down_out[rows] = own[rows].astype(jnp.bfloat16)
                down(c, rows).start()

        each_size(c, act_on)

    def climb(c):
        def act_on(rows, first, size):
            up(c, rows).wait_recv()

            @pl.when(g < last)
            def _():
                up_out[rows] = (own[rows] + up_in[rows].astype(jnp.float32)).astype(jnp.bfloat16)
                up(c, rows).start()

        each_size(c, act_on)

    def descend(c):
        def act_on(rows, first, size):
            down(c, rows).wait_recv()

            @pl.when(g > 0)
            def _():
                down_out[rows] = (own[rows] + down_in[rows].astype(jnp.float32)).astype(jnp.bfloat16)
                down(c, rows).start()

        each_size(c, act_on)

    def total(c):
        def act_on(rows, first, size):
            panel = own[rows] + up_in[rows].astype(jnp.float32) + down_in[rows].astype(jnp.float32)
            panel = panel.astype(jnp.bfloat16)
            rights[i, rows] = panel
            for k in range(1, nx):
                across_x(k, c, rows, i).start()
            for k in range(1, ncol):
                across_y(k, c, rows, j).start()
            to_sib(0, c, rows, i).start()
            lefts[j, rows] = panel

        each_size(c, act_on)

    def pass_on(c):
        def act_on(rows, first, size):
            for k in range(1, nx):
                row = ((x - k + nx) % nx) * 2 + core
                across_x(k, c, rows, row).wait_recv()
                to_sib(k, c, rows, row).start()

        each_size(c, act_on)

    def landed(c):
        def act_on(rows, first, size):
            for k in range(1, ncol):
                across_y(k, c, rows, (j - k + ncol) % ncol).wait_recv()
            to_sib(0, c, rows, x * 2 + 1 - core).wait_recv()
            for k in range(1, nx):
                to_sib(k, c, rows, ((x - k + nx) % nx) * 2 + 1 - core).wait_recv()

        each_size(c, act_on)

    def stack(b, final=False):
        start = b * DEPTH if final else pl.multiple_of(b * DEPTH, DEPTH)

        @pl.loop(0, ncol)
        def _(col):
            for r in range(nreg):
                lhs[col * nreg + r] = lefts[col, pl.ds(start, DEPTH), r * wide:(r + 1) * wide].T

        @pl.loop(0, nrow)
        def _(row):
            for r in range(nreg):
                lanes = slice(r * wide, (r + 1) * wide)
                for n in range(DEPTH // HALF):
                    at = start + n * HALF
                    rhs[row * nreg + r, n, :HALF] = rights[row, pl.ds(at, HALF), lanes]
                    now = rights[row, pl.ds(at, ahead), lanes]
                    if final and n == DEPTH // HALF - 1:
                        after = jnp.zeros_like(now)
                    else:
                        after = rights[row, pl.ds(at + HALF, ahead), lanes]
                    rhs[row * nreg + r, n, HALF:] = wrapped(now, after)

    def products(p):
        left, right = lhs[pairs_ref[0, p]], rhs[pairs_ref[1, p]]
        shifts = [
            jnp.concatenate([right[k, n * RUN:n * RUN + HALF] for k in range(DEPTH // HALF)], axis=0)
            for n in range(nlag // 2 + 1)
        ]
        return (
            jnp.dot(left, jnp.concatenate(shifts[:-1], axis=1), preferred_element_type=jnp.float32),
            jnp.dot(left[width:], shifts[-1], preferred_element_type=jnp.float32),
        )

    nstep = total_rows // DEPTH
    per = DEPTH // BIG
    share = npairs // per

    begin(0)
    begin(1)

    @pl.loop(0, npairs)
    def _(p):
        acc[p] = jnp.zeros(acc.shape[1:], jnp.float32)
        odd_acc[p] = jnp.zeros(odd_acc.shape[1:], jnp.float32)

    project(1)

    @pl.loop(0, ntile + HOP * last + CROSS + TURN)
    def _(s):
        @pl.when(g > 0)
        def _():
            climb(s - HOP * g)

        @pl.when(g < last)
        def _():
            descend(s - HOP * (last - g))

        done = s - HOP * jnp.maximum(g, last - g)
        total(done)
        pass_on(done - CROSS)
        begin(s + 2)

        @pl.when(jnp.logical_and(s % 2 == 0, s // 2 + 2 < nblock))
        def _():
            project(s // 2 + 2)

        here = done - CROSS - TURN
        landed(here)

        @pl.when(jnp.logical_and(here >= per, here < nstep * per))
        def _():
            @pl.when(here % per == 0)
            def _():
                stack(here // per - 1)

            for n in range(share):
                p = here % per * share + n
                even, odd = products(p)
                acc[p] += even
                odd_acc[p] += odd

    stack(nstep - 1, final=True)
    scale = 1.0 / bins**0.5
    half = lax.broadcasted_iota(jnp.int32, (width, wide), 1) < width
    for p in range(npairs):
        even, odd = products(p)
        even, odd = acc[p] + even, odd_acc[p] + odd
        upper = [even[width:, n * wide:(n + 1) * wide] for n in range(nlag // 2)] + [odd]
        upper = [pltpu.roll(part, width, 1) for part in upper]
        for n in range(nlag // 2):
            both = even[:width, n * wide:(n + 1) * wide] + jnp.where(half, upper[n], upper[n + 1])
            raw_ref[p, n] = (both * scale).astype(jnp.bfloat16)

    def finish(c):
        def act_on(rows, first, size):
            @pl.when(g < last)
            def _():
                up(c, rows).wait_send()

            @pl.when(g > 0)
            def _():
                down(c, rows).wait_send()

            for k in range(1, nx):
                across_x(k, c, rows, i).wait_send()
            for k in range(1, ncol):
                across_y(k, c, rows, j).wait_send()
            for k in range(nx):
                to_sib(k, c, rows, i).wait_send()

        each_size(c, act_on)

    @pl.loop(0, ntile)
    def _(c):
        finish(c)


def raw_covariances(shape, nlag, region_of, pairs, basis, activity):
    nrow, ncol, nreg = shape
    nx = nrow // 2
    width, neurons = basis.shape
    npairs = pairs.shape[1]
    bins = activity.shape[1]
    rows, lanes, wide = bins // 2, 2 * width * nreg, 2 * width
    ntile = (rows - NSMALL * SMALL) // BIG + NSMALL
    ahead = nlag // 2 * RUN
    dma = pltpu.SemaphoreType.DMA
    panel = pltpu.VMEM((rows, lanes), jnp.bfloat16)
    return pl.pallas_call(
        functools.partial(panels_kernel, shape, nlag),
        in_specs=[
            pl.BlockSpec(memory_space=pltpu.SMEM),
            pl.BlockSpec(memory_space=pltpu.SMEM),
            pl.BlockSpec(memory_space=pltpu.VMEM),
            pl.BlockSpec(memory_space=pltpu.HBM),
        ],
        out_specs=pl.BlockSpec(memory_space=pltpu.VMEM),
        out_shape=jax.ShapeDtypeStruct((npairs, nlag // 2, width, wide), jnp.bfloat16),
        scratch_shapes=[
            pltpu.VMEM((neurons, lanes), jnp.bfloat16),
            pltpu.VMEM((bins // SPAN, neurons, SPAN), jnp.bfloat16),
            pltpu.VMEM((nreg, SPAN, wide), jnp.float32),
            pltpu.VMEM((rows, lanes), jnp.float32),
            panel, panel, panel, panel,
            pltpu.VMEM((ncol, rows, lanes), jnp.bfloat16),
            pltpu.VMEM((nrow, rows, lanes), jnp.bfloat16),
            pltpu.VMEM((ncol * nreg, wide, DEPTH), jnp.bfloat16),
            pltpu.VMEM((nrow * nreg, DEPTH // HALF, HALF + ahead, wide), jnp.bfloat16),
            pltpu.VMEM((npairs, wide, nlag * width), jnp.float32),
            pltpu.VMEM((npairs, width, wide), jnp.float32),
            dma((bins // SPAN,)),
        ]
        + [dma((ntile,))] * 4
        + [dma((nx - 1, ntile))] * 2
        + [dma((ncol - 1, ntile))] * 2
        + [dma((nx, ntile))] * 2,
        compiler_params=pltpu.CompilerParams(
            collective_id=0, has_side_effects=True, vmem_limit_bytes=60 << 20
        ),
    )(region_of, pairs, basis, activity)


def order_kernel(lags_ref, raw_ref, out_ref):
    group, width, _ = out_ref.shape
    low = lax.broadcasted_iota(jnp.int32, (width, 2 * width), 1) < width
    for q in range(group):
        for s in range(lags_ref.shape[0] // 2):
            first, second = lags_ref[2 * s], lags_ref[2 * s + 1]
            a, b = raw_ref[q, first // 2], raw_ref[q, second // 2]
            a = jnp.where(first % 2 == 0, a, pltpu.roll(a, width, 1))
            b = jnp.where(second % 2 == 0, pltpu.roll(b, width, 1), b)
            out_ref[q, :, s * 2 * width:(s + 1) * 2 * width] = jnp.where(low, a, b)


def ordered(raw, lags):
    npairs, halves, width, wide = raw.shape
    group = 8
    return pl.pallas_call(
        order_kernel,
        grid=(npairs // group,),
        in_specs=[
            pl.BlockSpec(memory_space=pltpu.SMEM),
            pl.BlockSpec((group, halves, width, wide), lambda p: (p, 0, 0, 0)),
        ],
        out_specs=pl.BlockSpec((group, width, halves * wide), lambda p: (p, 0, 0)),
        out_shape=jax.ShapeDtypeStruct((npairs, width, halves * wide), jnp.bfloat16),
    )(lags, raw)


def local(shape, activity, basis, region_of, pairs, lags):
    raw = raw_covariances(shape, lags.shape[0], region_of, pairs.T, basis.T, activity)
    return ordered(raw, lags)


def solution(mesh):
    shape = (mesh.shape["row"], mesh.shape["col"], mesh.shape["reg"])
    return jax.shard_map(
        functools.partial(local, shape),
        mesh=mesh,
        in_specs=(
            P(("row", "col", "reg"), None),
            P(("row", "col", "reg"), None),
            P(("row", "col", "reg")),
            P(("row", "col", "reg"), None),
            P(),
        ),
        out_specs=P(("row", "col", "reg"), None, None),
        check_vma=False,
    )
```

```python
import functools

import jax
import jax.numpy as jnp
from jax import lax
from jax.experimental import pallas as pl
from jax.experimental.pallas import tpu as pltpu
from jax.sharding import PartitionSpec as P

BLK = 128
PHASES = 16
RUN = 16
SPAN = PHASES * RUN
HALF = SPAN // 2
BIG, SMALL = 64, 32
NSMALL = 4
DEPTH = 256
HOP = 3
CROSS = 4
TURN = 2


def wrapped(now, after):
    rows = now.shape[0]
    at = lax.broadcasted_iota(jnp.int32, now.shape, 0) % RUN
    moved = pltpu.roll(now.astype(jnp.float32), rows - 1, 0)
    missing = pltpu.roll(after.astype(jnp.float32), RUN - 1, 0)
    return jnp.where(at == RUN - 1, missing, moved).astype(jnp.bfloat16)


def panels_kernel(
    shape, nlag, region_hbm, pairs_hbm, basis_hbm, act_ref, raw_hbm,
    region_ref, pairs_ref, basis_ref, raw_ref, masked, act, natural, own, up_in, down_in, up_out, down_out, lefts, rights, lhs, rhs, acc, odd_acc,
    region_sem, pairs_sem, basis_sem, raw_sem, act_sem, up_send, up_recv, down_send, down_recv,
    x_send, x_recv, y_send, y_recv, sib_send, sib_recv,
):
    nrow, ncol, nreg = shape
    nx = nrow // 2
    width, neurons = basis_hbm.shape
    wide = 2 * width
    npairs = acc.shape[0]
    nblock = act.shape[0]
    bins = nblock * SPAN
    total_rows = bins // 2
    nbig = (total_rows - NSMALL * SMALL) // BIG
    ntile = nbig + NSMALL
    ahead = nlag // 2 * RUN
    i, j, g = lax.axis_index("row"), lax.axis_index("col"), lax.axis_index("reg")
    x, core = i // 2, i % 2
    sib = {"row": x * 2 + 1 - core}
    last = nreg - 1

    def x_row(k):
        return ((x + k) % nx) * 2 + core

    def col_at(k):
        return (j + k) % ncol

    def load(b):
        return pltpu.make_async_copy(
            act_ref.at[:, pl.ds(pl.multiple_of(b * SPAN, SPAN), SPAN)], act.at[b], act_sem.at[b]
        )

    basis_load = pltpu.make_async_copy(basis_hbm, basis_ref, basis_sem)
    region_load = pltpu.make_async_copy(region_hbm, region_ref, region_sem)
    pairs_load = pltpu.make_async_copy(pairs_hbm, pairs_ref, pairs_sem)
    barrier = pltpu.get_barrier_semaphore()

    def greet(peer):
        pl.semaphore_signal(barrier, inc=1, device_id=peer, device_id_type=pl.DeviceIdType.MESH)

    @pl.when(g > 0)
    def _():
        greet({"reg": g - 1})

    @pl.when(g < last)
    def _():
        greet({"reg": g + 1})

    for k in range(1, nx):
        greet({"row": x_row(k)})
    for k in range(1, ncol):
        greet({"col": col_at(k)})
    greet(sib)

    def remote(src, dst, send_sem, recv_sem, peer):
        return pltpu.make_async_remote_copy(
            src_ref=src, dst_ref=dst, send_sem=send_sem, recv_sem=recv_sem,
            device_id=peer, device_id_type=pl.DeviceIdType.MESH,
        )

    def up(c, rows):
        return remote(up_out.at[rows], up_in.at[rows], up_send.at[c], up_recv.at[c], {"reg": g + 1})

    def down(c, rows):
        return remote(down_out.at[rows], down_in.at[rows], down_send.at[c], down_recv.at[c], {"reg": g - 1})

    def across_x(k, c, rows, row):
        here = rights.at[row, rows]
        return remote(here, here, x_send.at[k - 1, c], x_recv.at[k - 1, c], {"row": x_row(k)})

    def across_y(k, c, rows, col):
        return remote(
            rights.at[i, rows], lefts.at[col, rows], y_send.at[k - 1, c], y_recv.at[k - 1, c],
            {"col": col_at(k)},
        )

    def to_sib(k, c, rows, row):
        here = rights.at[row, rows]
        return remote(here, here, sib_send.at[k, c], sib_recv.at[k, c], sib)

    region_load.start()
    basis_load.start()
    pairs_load.start()

    @pl.loop(0, nblock)
    def _(b):
        load(b).start()

    region_load.wait()
    basis_load.wait()
    pairs_load.wait()
    for n in range(neurons // BLK):
        block = basis_ref[:, n * BLK:(n + 1) * BLK].T
        masked[n * BLK:(n + 1) * BLK, :] = jnp.concatenate(
            [jnp.where(region_ref[n] == r // 2, block, jnp.zeros_like(block)) for r in range(2 * nreg)], axis=1
        )

    low = lax.broadcasted_iota(jnp.int32, (RUN, wide), 1) < width

    def project(b):
        load(b).wait()
        part = lax.dot_general(
            act[b], masked[...], (((0,), (0,)), ((), ())), preferred_element_type=jnp.float32
        )
        for r in range(nreg):
            natural[r] = part[:, r * wide:(r + 1) * wide]
        for n in range(HALF // RUN):
            rows = pl.ds(pl.multiple_of(b * HALF + n * RUN, RUN), RUN)
            for r in range(nreg):
                own[rows, r * wide:(r + 1) * wide] = jnp.where(
                    low,
                    natural[r, pl.ds(2 * n, RUN, stride=PHASES), :],
                    natural[r, pl.ds(2 * n + 1, RUN, stride=PHASES), :],
                )

    project(0)
    ends = jnp.where(jnp.logical_or(g == 0, g == last), 1, 2)
    pl.semaphore_wait(barrier, ends + nx + ncol - 1)

    def each_size(c, act_on):
        @pl.when(jnp.logical_and(c >= 0, c < nbig))
        def _():
            first = pl.multiple_of(c * BIG, BIG)
            act_on(pl.ds(first, BIG), first, BIG)

        @pl.when(jnp.logical_and(c >= nbig, c < ntile))
        def _():
            first = pl.multiple_of(nbig * BIG + (c - nbig) * SMALL, SMALL)
            act_on(pl.ds(first, SMALL), first, SMALL)

    def begin(c):
        def act_on(rows, first, size):
            @pl.when(g == 0)
            def _():
                up_out[rows] = own[rows].astype(jnp.bfloat16)
                up(c, rows).start()

            @pl.when(g == last)
            def _():
                down_out[rows] = own[rows].astype(jnp.bfloat16)
                down(c, rows).start()

        each_size(c, act_on)

    def climb(c):
        def act_on(rows, first, size):
            up(c, rows).wait_recv()

            @pl.when(g < last)
            def _():
                up_out[rows] = (own[rows] + up_in[rows].astype(jnp.float32)).astype(jnp.bfloat16)
                up(c, rows).start()

        each_size(c, act_on)

    def descend(c):
        def act_on(rows, first, size):
            down(c, rows).wait_recv()

            @pl.when(g > 0)
            def _():
                down_out[rows] = (own[rows] + down_in[rows].astype(jnp.float32)).astype(jnp.bfloat16)
                down(c, rows).start()

        each_size(c, act_on)

    def total(c):
        def act_on(rows, first, size):
            panel = own[rows] + up_in[rows].astype(jnp.float32) + down_in[rows].astype(jnp.float32)
            panel = panel.astype(jnp.bfloat16)
            rights[i, rows] = panel
            for k in range(1, nx):
                across_x(k, c, rows, i).start()
            for k in range(1, ncol):
                across_y(k, c, rows, j).start()
            to_sib(0, c, rows, i).start()
            lefts[j, rows] = panel

        each_size(c, act_on)

    def pass_on(c):
        def act_on(rows, first, size):
            for k in range(1, nx):
                row = ((x - k + nx) % nx) * 2 + core
                across_x(k, c, rows, row).wait_recv()
                to_sib(k, c, rows, row).start()

        each_size(c, act_on)

    def landed(c):
        def act_on(rows, first, size):
            for k in range(1, ncol):
                across_y(k, c, rows, (j - k + ncol) % ncol).wait_recv()
            to_sib(0, c, rows, x * 2 + 1 - core).wait_recv()
            for k in range(1, nx):
                to_sib(k, c, rows, ((x - k + nx) % nx) * 2 + 1 - core).wait_recv()

        each_size(c, act_on)

    def stack(b, final=False):
        start = b * DEPTH if final else pl.multiple_of(b * DEPTH, DEPTH)

        @pl.loop(0, ncol)
        def _(col):
            for r in range(nreg):
                lhs[col * nreg + r] = lefts[col, pl.ds(start, DEPTH), r * wide:(r + 1) * wide].T

        @pl.loop(0, nrow)
        def _(row):
            for r in range(nreg):
                lanes = slice(r * wide, (r + 1) * wide)
                for n in range(DEPTH // HALF):
                    at = start + n * HALF
                    rhs[row * nreg + r, n, :HALF] = rights[row, pl.ds(at, HALF), lanes]
                    now = rights[row, pl.ds(at, ahead), lanes]
                    if final and n == DEPTH // HALF - 1:
                        after = jnp.zeros_like(now)
                    else:
                        after = rights[row, pl.ds(at + HALF, ahead), lanes]
                    rhs[row * nreg + r, n, HALF:] = wrapped(now, after)

    def products(p):
        left, right = lhs[pairs_ref[0, p]], rhs[pairs_ref[1, p]]
        shifts = [
            jnp.concatenate([right[k, n * RUN:n * RUN + HALF] for k in range(DEPTH // HALF)], axis=0)
            for n in range(nlag // 2 + 1)
        ]
        return (
            jnp.dot(left, jnp.concatenate(shifts[:-1], axis=1), preferred_element_type=jnp.float32),
            jnp.dot(left[width:], shifts[-1], preferred_element_type=jnp.float32),
        )

    nstep = total_rows // DEPTH
    per = DEPTH // BIG
    share = npairs // per

    begin(0)
    begin(1)

    @pl.when(g == 0)
    def _():
        up_in[...] = jnp.zeros_like(up_in)

    @pl.when(g == last)
    def _():
        down_in[...] = jnp.zeros_like(down_in)

    @pl.loop(0, npairs)
    def _(p):
        acc[p] = jnp.zeros(acc.shape[1:], jnp.float32)
        odd_acc[p] = jnp.zeros(odd_acc.shape[1:], jnp.float32)

    project(1)

    @pl.loop(0, ntile + HOP * last + CROSS + TURN)
    def _(s):
        @pl.when(g > 0)
        def _():
            climb(s - HOP * g)

        @pl.when(g < last)
        def _():
            descend(s - HOP * (last - g))

        done = s - HOP * jnp.maximum(g, last - g)
        total(done)
        pass_on(done - CROSS)
        begin(s + 2)

        @pl.when(jnp.logical_and(s % 2 == 0, s // 2 + 2 < nblock))
        def _():
            project(s // 2 + 2)

        here = done - CROSS - TURN
        landed(here)

        @pl.when(jnp.logical_and(here >= per, here < nstep * per))
        def _():
            @pl.when(here % per == 0)
            def _():
                stack(here // per - 1)

            for n in range(share):
                p = here % per * share + n
                even, odd = products(p)
                acc[p] += even
                odd_acc[p] += odd

    stack(nstep - 1, final=True)
    scale = 1.0 / bins**0.5
    half = lax.broadcasted_iota(jnp.int32, (width, wide), 1) < width
    group = npairs // raw_sem.shape[0]

    def store(q):
        rows = pl.ds(q * group * width, group * width)
        return pltpu.make_async_copy(raw_ref.at[rows], raw_hbm.at[rows], raw_sem.at[q])

    for p in range(npairs):
        even, odd = products(p)
        even, odd = acc[p] + even, odd_acc[p] + odd
        upper = [even[width:, n * wide:(n + 1) * wide] for n in range(nlag // 2)] + [odd]
        upper = [pltpu.roll(part, width, 1) for part in upper]
        for n in range(nlag // 2):
            both = even[:width, n * wide:(n + 1) * wide] + jnp.where(half, upper[n], upper[n + 1])
            raw_ref[p * width:(p + 1) * width, n * wide:(n + 1) * wide] = (both * scale).astype(jnp.bfloat16)
        if p % group == group - 1:
            store(p // group).start()

    def finish(c):
        def act_on(rows, first, size):
            @pl.when(g < last)
            def _():
                up(c, rows).wait_send()

            @pl.when(g > 0)
            def _():
                down(c, rows).wait_send()

            for k in range(1, nx):
                across_x(k, c, rows, i).wait_send()
            for k in range(1, ncol):
                across_y(k, c, rows, j).wait_send()
            for k in range(nx):
                to_sib(k, c, rows, i).wait_send()

        each_size(c, act_on)

    @pl.loop(0, ntile)
    def _(c):
        finish(c)

    for q in range(npairs // group):
        store(q).wait()


def raw_covariances(shape, nlag, region_of, pairs, basis, activity):
    nrow, ncol, nreg = shape
    nx = nrow // 2
    width, neurons = basis.shape
    npairs = pairs.shape[1]
    bins = activity.shape[1]
    rows, lanes, wide = bins // 2, 2 * width * nreg, 2 * width
    ntile = (rows - NSMALL * SMALL) // BIG + NSMALL
    ahead = nlag // 2 * RUN
    dma = pltpu.SemaphoreType.DMA
    panel = pltpu.VMEM((rows, lanes), jnp.bfloat16)
    return pl.pallas_call(
        functools.partial(panels_kernel, shape, nlag),
        in_specs=[
            pl.BlockSpec(memory_space=pltpu.HBM),
            pl.BlockSpec(memory_space=pltpu.HBM),
            pl.BlockSpec(memory_space=pltpu.HBM),
            pl.BlockSpec(memory_space=pltpu.HBM),
        ],
        out_specs=pl.BlockSpec(memory_space=pl.ANY),
        out_shape=jax.ShapeDtypeStruct((npairs * width, nlag * width), jnp.bfloat16),
        scratch_shapes=[
            pltpu.SMEM(region_of.shape, jnp.int32),
            pltpu.SMEM(pairs.shape, jnp.int32),
            pltpu.VMEM(basis.shape, jnp.bfloat16),
            pltpu.VMEM((npairs * width, nlag * width), jnp.bfloat16),
            pltpu.VMEM((neurons, lanes), jnp.bfloat16),
            pltpu.VMEM((bins // SPAN, neurons, SPAN), jnp.bfloat16),
            pltpu.VMEM((nreg, SPAN, wide), jnp.float32),
            pltpu.VMEM((rows, lanes), jnp.float32),
            panel, panel, panel, panel,
            pltpu.VMEM((ncol, rows, lanes), jnp.bfloat16),
            pltpu.VMEM((nrow, rows, lanes), jnp.bfloat16),
            pltpu.VMEM((ncol * nreg, wide, DEPTH), jnp.bfloat16),
            pltpu.VMEM((nrow * nreg, DEPTH // HALF, HALF + ahead, wide), jnp.bfloat16),
            pltpu.VMEM((npairs, wide, nlag * width), jnp.float32),
            pltpu.VMEM((npairs, width, wide), jnp.float32),
            dma,
            dma,
            dma,
            dma((4,)),
            dma((bins // SPAN,)),
        ]
        + [dma((ntile,))] * 4
        + [dma((nx - 1, ntile))] * 2
        + [dma((ncol - 1, ntile))] * 2
        + [dma((nx, ntile))] * 2,
        compiler_params=pltpu.CompilerParams(
            collective_id=0, has_side_effects=True, vmem_limit_bytes=60 << 20
        ),
    )(region_of, pairs, basis, activity)


def order_kernel(lags_hbm, raw_ref, out_ref, lags_ref, place, given, result, lags_sem, in_sem, sem):
    nlag, side = lags_ref.shape[0], raw_ref.shape[1]
    width = side // nlag
    parts = sem.shape[0]
    size = raw_ref.shape[0] // parts

    def load(n):
        rows = pl.ds(n * size, size)
        return pltpu.make_async_copy(raw_ref.at[rows], given.at[rows], in_sem.at[n])

    def store(n):
        rows = pl.ds(n * size, size)
        return pltpu.make_async_copy(result.at[rows], out_ref.at[rows], sem.at[n])

    lags_load = pltpu.make_async_copy(lags_hbm, lags_ref, lags_sem)
    lags_load.start()
    for n in range(parts):
        load(n).start()
    lags_load.wait()
    shift = lax.broadcasted_iota(jnp.int32, (side, width), 0) - lax.broadcasted_iota(jnp.int32, (side, width), 1)
    for m in range(nlag):
        place[:, m * width:(m + 1) * width] = jnp.where(shift == lags_ref[m] * width, 1.0, 0.0).astype(jnp.bfloat16)
    for n in range(parts):
        load(n).wait()
        rows = slice(n * size, (n + 1) * size)
        result[rows] = jnp.dot(given[rows], place[...], preferred_element_type=jnp.float32).astype(jnp.bfloat16)
        store(n).start()
    for n in range(parts):
        store(n).wait()


def ordered(raw, lags):
    total, side = raw.shape
    parts = 2
    return pl.pallas_call(
        order_kernel,
        in_specs=[pl.BlockSpec(memory_space=pl.ANY)] * 2,
        out_specs=pl.BlockSpec(memory_space=pl.ANY),
        out_shape=jax.ShapeDtypeStruct((total, side), jnp.bfloat16),
        scratch_shapes=[
            pltpu.SMEM(lags.shape, jnp.int32),
            pltpu.VMEM((side, side), jnp.bfloat16),
            pltpu.VMEM((total, side), jnp.bfloat16),
            pltpu.VMEM((total, side), jnp.bfloat16),
            pltpu.SemaphoreType.DMA,
            pltpu.SemaphoreType.DMA((parts,)),
            pltpu.SemaphoreType.DMA((parts,)),
        ],
    )(lags, raw)


def local(shape, activity, basis, region_of, pairs, lags):
    raw = raw_covariances(shape, lags.shape[0], region_of, pairs.T, basis.T, activity)
    return ordered(raw, lags).reshape(pairs.shape[0], basis.shape[1], -1)


def solution(mesh):
    shape = (mesh.shape["row"], mesh.shape["col"], mesh.shape["reg"])
    return jax.shard_map(
        functools.partial(local, shape),
        mesh=mesh,
        in_specs=(
            P(("row", "col", "reg"), None),
            P(("row", "col", "reg"), None),
            P(("row", "col", "reg")),
            P(("row", "col", "reg"), None),
            P(),
        ),
        out_specs=P(("row", "col", "reg"), None, None),
        check_vma=False,
    )
```

```python
import functools

import jax
import jax.numpy as jnp
from jax import lax
from jax.experimental import pallas as pl
from jax.experimental.pallas import tpu as pltpu
from jax.sharding import PartitionSpec as P

BLK = 128
PHASES = 16
RUN = 16
SPAN = PHASES * RUN
HALF = SPAN // 2
BIG, SMALL = 64, 32
NSMALL = 4
DEPTH = 256
HOP = 3
CROSS = 4
TURN = 2


def wrapped(now, after):
    rows = now.shape[0]
    at = lax.broadcasted_iota(jnp.int32, now.shape, 0) % RUN
    moved = pltpu.roll(now.astype(jnp.float32), rows - 1, 0)
    missing = pltpu.roll(after.astype(jnp.float32), RUN - 1, 0)
    return jnp.where(at == RUN - 1, missing, moved).astype(jnp.bfloat16)


def panels_kernel(
    shape, nlag, region_hbm, pairs_hbm, basis_hbm, act_ref, raw_hbm,
    region_ref, pairs_ref, basis_ref, raw_ref, masked, act, natural, own, up_in, down_in, up_out, down_out, lefts, rights, lhs, rhs, acc, odd_acc,
    region_sem, pairs_sem, basis_sem, raw_sem, act_sem, up_send, up_recv, down_send, down_recv,
    x_send, x_recv, y_send, y_recv, sib_send, sib_recv,
):
    nrow, ncol, nreg = shape
    nx = nrow // 2
    width, neurons = basis_hbm.shape
    wide = 2 * width
    npairs = acc.shape[0]
    nblock = act.shape[0]
    bins = nblock * SPAN
    total_rows = bins // 2
    nbig = (total_rows - NSMALL * SMALL) // BIG
    ntile = nbig + NSMALL
    ahead = nlag // 2 * RUN
    i, j, g = lax.axis_index("row"), lax.axis_index("col"), lax.axis_index("reg")
    x, core = i // 2, i % 2
    sib = {"row": x * 2 + 1 - core}
    last = nreg - 1

    def x_row(k):
        return ((x + k) % nx) * 2 + core

    def col_at(k):
        return (j + k) % ncol

    def load(b):
        return pltpu.make_async_copy(
            act_ref.at[:, pl.ds(pl.multiple_of(b * SPAN, SPAN), SPAN)], act.at[b], act_sem.at[b]
        )

    basis_load = pltpu.make_async_copy(basis_hbm, basis_ref, basis_sem)
    region_load = pltpu.make_async_copy(region_hbm, region_ref, region_sem)
    pairs_load = pltpu.make_async_copy(pairs_hbm, pairs_ref, pairs_sem)
    barrier = pltpu.get_barrier_semaphore()

    def greet(peer):
        pl.semaphore_signal(barrier, inc=1, device_id=peer, device_id_type=pl.DeviceIdType.MESH)

    @pl.when(g > 0)
    def _():
        greet({"reg": g - 1})

    @pl.when(g < last)
    def _():
        greet({"reg": g + 1})

    for k in range(1, nx):
        greet({"row": x_row(k)})
    for k in range(1, ncol):
        greet({"col": col_at(k)})
    greet(sib)

    def remote(src, dst, send_sem, recv_sem, peer):
        return pltpu.make_async_remote_copy(
            src_ref=src, dst_ref=dst, send_sem=send_sem, recv_sem=recv_sem,
            device_id=peer, device_id_type=pl.DeviceIdType.MESH,
        )

    def up(c, rows):
        return remote(up_out.at[rows], up_in.at[rows], up_send.at[c], up_recv.at[c], {"reg": g + 1})

    def down(c, rows):
        return remote(down_out.at[rows], down_in.at[rows], down_send.at[c], down_recv.at[c], {"reg": g - 1})

    def across_x(k, c, rows, row):
        here = rights.at[row, rows]
        return remote(here, here, x_send.at[k - 1, c], x_recv.at[k - 1, c], {"row": x_row(k)})

    def across_y(k, c, rows, col):
        return remote(
            rights.at[i, rows], lefts.at[col, rows], y_send.at[k - 1, c], y_recv.at[k - 1, c],
            {"col": col_at(k)},
        )

    def to_sib(k, c, rows, row):
        here = rights.at[row, rows]
        return remote(here, here, sib_send.at[k, c], sib_recv.at[k, c], sib)

    region_load.start()
    basis_load.start()
    pairs_load.start()

    @pl.loop(0, nblock)
    def _(b):
        load(b).start()

    region_load.wait()
    basis_load.wait()
    pairs_load.wait()
    for n in range(neurons // BLK):
        block = basis_ref[:, n * BLK:(n + 1) * BLK].T
        masked[n * BLK:(n + 1) * BLK, :] = jnp.concatenate(
            [jnp.where(region_ref[n] == r // 2, block, jnp.zeros_like(block)) for r in range(2 * nreg)], axis=1
        )

    low = lax.broadcasted_iota(jnp.int32, (RUN, wide), 1) < width

    def project(b):
        load(b).wait()
        part = lax.dot_general(
            act[b], masked[...], (((0,), (0,)), ((), ())), preferred_element_type=jnp.float32
        )
        for r in range(nreg):
            natural[r] = part[:, r * wide:(r + 1) * wide]
        for n in range(HALF // RUN):
            rows = pl.ds(pl.multiple_of(b * HALF + n * RUN, RUN), RUN)
            for r in range(nreg):
                own[rows, r * wide:(r + 1) * wide] = jnp.where(
                    low,
                    natural[r, pl.ds(2 * n, RUN, stride=PHASES), :],
                    natural[r, pl.ds(2 * n + 1, RUN, stride=PHASES), :],
                )

    project(0)
    ends = jnp.where(jnp.logical_or(g == 0, g == last), 1, 2)
    pl.semaphore_wait(barrier, ends + nx + ncol - 1)

    def each_size(c, act_on):
        @pl.when(jnp.logical_and(c >= 0, c < nbig))
        def _():
            first = pl.multiple_of(c * BIG, BIG)
            act_on(pl.ds(first, BIG), first, BIG)

        @pl.when(jnp.logical_and(c >= nbig, c < ntile))
        def _():
            first = pl.multiple_of(nbig * BIG + (c - nbig) * SMALL, SMALL)
            act_on(pl.ds(first, SMALL), first, SMALL)

    def begin(c):
        def act_on(rows, first, size):
            @pl.when(g == 0)
            def _():
                up_out[rows] = own[rows].astype(jnp.bfloat16)
                up(c, rows).start()

            @pl.when(g == last)
            def _():
                down_out[rows] = own[rows].astype(jnp.bfloat16)
                down(c, rows).start()

        each_size(c, act_on)

    def climb(c):
        def act_on(rows, first, size):
            up(c, rows).wait_recv()

            @pl.when(g < last)
            def _():
                up_out[rows] = (own[rows] + up_in[rows].astype(jnp.float32)).astype(jnp.bfloat16)
                up(c, rows).start()

        each_size(c, act_on)

    def descend(c):
        def act_on(rows, first, size):
            down(c, rows).wait_recv()

            @pl.when(g > 0)
            def _():
                down_out[rows] = (own[rows] + down_in[rows].astype(jnp.float32)).astype(jnp.bfloat16)
                down(c, rows).start()

        each_size(c, act_on)

    def total(c):
        def act_on(rows, first, size):
            panel = own[rows] + up_in[rows].astype(jnp.float32) + down_in[rows].astype(jnp.float32)
            panel = panel.astype(jnp.bfloat16)
            rights[i, rows] = panel
            for k in range(1, nx):
                across_x(k, c, rows, i).start()
            for k in range(1, ncol):
                across_y(k, c, rows, j).start()
            to_sib(0, c, rows, i).start()
            lefts[j, rows] = panel

        each_size(c, act_on)

    def pass_on(c):
        def act_on(rows, first, size):
            for k in range(1, nx):
                row = ((x - k + nx) % nx) * 2 + core
                across_x(k, c, rows, row).wait_recv()
                to_sib(k, c, rows, row).start()

        each_size(c, act_on)

    def landed(c):
        def act_on(rows, first, size):
            for k in range(1, ncol):
                across_y(k, c, rows, (j - k + ncol) % ncol).wait_recv()
            to_sib(0, c, rows, x * 2 + 1 - core).wait_recv()
            for k in range(1, nx):
                to_sib(k, c, rows, ((x - k + nx) % nx) * 2 + 1 - core).wait_recv()

        each_size(c, act_on)

    nstep = total_rows // DEPTH

    def stack_half(n):
        start = (nstep - 1) * DEPTH + n * HALF

        @pl.loop(0, ncol)
        def _(col):
            for r in range(nreg):
                block = lefts[col, start:start + HALF, r * wide:(r + 1) * wide]
                lhs[col * nreg + r, :, n * HALF:(n + 1) * HALF] = block.T

        @pl.loop(0, nrow)
        def _(row):
            for r in range(nreg):
                lanes = slice(r * wide, (r + 1) * wide)
                rhs[row * nreg + r, n, :HALF] = rights[row, start:start + HALF, lanes]
                now = rights[row, start:start + ahead, lanes]
                if start + HALF == total_rows:
                    after = jnp.zeros_like(now)
                else:
                    after = rights[row, start + HALF:start + HALF + ahead, lanes]
                rhs[row * nreg + r, n, HALF:] = wrapped(now, after)

    def stack(b):
        start = pl.multiple_of(b * DEPTH, DEPTH)

        @pl.loop(0, ncol)
        def _(col):
            for r in range(nreg):
                lhs[col * nreg + r] = lefts[col, pl.ds(start, DEPTH), r * wide:(r + 1) * wide].T

        @pl.loop(0, nrow)
        def _(row):
            for r in range(nreg):
                lanes = slice(r * wide, (r + 1) * wide)
                for n in range(DEPTH // HALF):
                    at = start + n * HALF
                    rhs[row * nreg + r, n, :HALF] = rights[row, pl.ds(at, HALF), lanes]
                    now = rights[row, pl.ds(at, ahead), lanes]
                    after = rights[row, pl.ds(at + HALF, ahead), lanes]
                    rhs[row * nreg + r, n, HALF:] = wrapped(now, after)

    def products(p):
        left, right = lhs[pairs_ref[0, p]], rhs[pairs_ref[1, p]]
        shifts = [
            jnp.concatenate([right[k, n * RUN:n * RUN + HALF] for k in range(DEPTH // HALF)], axis=0)
            for n in range(nlag // 2 + 1)
        ]
        full = jnp.dot(left, jnp.concatenate(shifts[2:], axis=1), preferred_element_type=jnp.float32)
        first = jnp.dot(left, jnp.concatenate(shifts[:2], axis=1), preferred_element_type=jnp.float32)
        return jnp.concatenate([first, full[:, :2 * wide]], axis=1), full[width:, 2 * wide:]

    per = DEPTH // BIG
    share = npairs // per

    begin(0)
    begin(1)

    @pl.when(g == 0)
    def _():
        up_in[...] = jnp.zeros_like(up_in)

    @pl.when(g == last)
    def _():
        down_in[...] = jnp.zeros_like(down_in)

    @pl.loop(0, npairs)
    def _(p):
        acc[p] = jnp.zeros(acc.shape[1:], jnp.float32)
        odd_acc[p] = jnp.zeros(odd_acc.shape[1:], jnp.float32)

    project(1)

    @pl.loop(0, ntile + HOP * last + CROSS + TURN)
    def _(s):
        @pl.when(g > 0)
        def _():
            climb(s - HOP * g)

        @pl.when(g < last)
        def _():
            descend(s - HOP * (last - g))

        done = s - HOP * jnp.maximum(g, last - g)
        total(done)
        pass_on(done - CROSS)
        begin(s + 2)

        @pl.when(jnp.logical_and(s % 2 == 0, s // 2 + 2 < nblock))
        def _():
            project(s // 2 + 2)

        here = done - CROSS - TURN
        landed(here)

        @pl.when(jnp.logical_and(here >= per, here < nstep * per))
        def _():
            @pl.when(here % per == 0)
            def _():
                stack(here // per - 1)

            for n in range(share):
                p = here % per * share + n
                even, odd = products(p)
                acc[p] += even
                odd_acc[p] += odd

        @pl.when(here == nstep * per)
        def _():
            stack_half(0)

    for n in range(1, DEPTH // HALF):
        stack_half(n)
    scale = 1.0 / bins**0.5
    half = lax.broadcasted_iota(jnp.int32, (width, wide), 1) < width
    group = npairs // raw_sem.shape[0]

    def store(q):
        rows = pl.ds(q * group * width, group * width)
        return pltpu.make_async_copy(raw_ref.at[rows], raw_hbm.at[rows], raw_sem.at[q])

    for p in range(npairs):
        even, odd = products(p)
        even, odd = acc[p] + even, odd_acc[p] + odd
        upper = [even[width:, n * wide:(n + 1) * wide] for n in range(nlag // 2)] + [odd]
        upper = [pltpu.roll(part, width, 1) for part in upper]
        for n in range(nlag // 2):
            both = even[:width, n * wide:(n + 1) * wide] + jnp.where(half, upper[n], upper[n + 1])
            raw_ref[p * width:(p + 1) * width, n * wide:(n + 1) * wide] = (both * scale).astype(jnp.bfloat16)
        if p % group == group - 1:
            store(p // group).start()

    def finish(c):
        def act_on(rows, first, size):
            @pl.when(g < last)
            def _():
                up(c, rows).wait_send()

            @pl.when(g > 0)
            def _():
                down(c, rows).wait_send()

            for k in range(1, nx):
                across_x(k, c, rows, i).wait_send()
            for k in range(1, ncol):
                across_y(k, c, rows, j).wait_send()
            for k in range(nx):
                to_sib(k, c, rows, i).wait_send()

        each_size(c, act_on)

    @pl.loop(0, ntile)
    def _(c):
        finish(c)

    for q in range(npairs // group):
        store(q).wait()


def raw_covariances(shape, nlag, region_of, pairs, basis, activity):
    nrow, ncol, nreg = shape
    nx = nrow // 2
    width, neurons = basis.shape
    npairs = pairs.shape[1]
    bins = activity.shape[1]
    rows, lanes, wide = bins // 2, 2 * width * nreg, 2 * width
    ntile = (rows - NSMALL * SMALL) // BIG + NSMALL
    ahead = nlag // 2 * RUN
    dma = pltpu.SemaphoreType.DMA
    panel = pltpu.VMEM((rows, lanes), jnp.bfloat16)
    return pl.pallas_call(
        functools.partial(panels_kernel, shape, nlag),
        in_specs=[
            pl.BlockSpec(memory_space=pltpu.HBM),
            pl.BlockSpec(memory_space=pltpu.HBM),
            pl.BlockSpec(memory_space=pltpu.HBM),
            pl.BlockSpec(memory_space=pltpu.HBM),
        ],
        out_specs=pl.BlockSpec(memory_space=pl.ANY),
        out_shape=jax.ShapeDtypeStruct((npairs * width, nlag * width), jnp.bfloat16),
        scratch_shapes=[
            pltpu.SMEM(region_of.shape, jnp.int32),
            pltpu.SMEM(pairs.shape, jnp.int32),
            pltpu.VMEM(basis.shape, jnp.bfloat16),
            pltpu.VMEM((npairs * width, nlag * width), jnp.bfloat16),
            pltpu.VMEM((neurons, lanes), jnp.bfloat16),
            pltpu.VMEM((bins // SPAN, neurons, SPAN), jnp.bfloat16),
            pltpu.VMEM((nreg, SPAN, wide), jnp.float32),
            pltpu.VMEM((rows, lanes), jnp.float32),
            panel, panel, panel, panel,
            pltpu.VMEM((ncol, rows, lanes), jnp.bfloat16),
            pltpu.VMEM((nrow, rows, lanes), jnp.bfloat16),
            pltpu.VMEM((ncol * nreg, wide, DEPTH), jnp.bfloat16),
            pltpu.VMEM((nrow * nreg, DEPTH // HALF, HALF + ahead, wide), jnp.bfloat16),
            pltpu.VMEM((npairs, wide, nlag * width), jnp.float32),
            pltpu.VMEM((npairs, width, wide), jnp.float32),
            dma,
            dma,
            dma,
            dma((4,)),
            dma((bins // SPAN,)),
        ]
        + [dma((ntile,))] * 4
        + [dma((nx - 1, ntile))] * 2
        + [dma((ncol - 1, ntile))] * 2
        + [dma((nx, ntile))] * 2,
        compiler_params=pltpu.CompilerParams(
            collective_id=0, has_side_effects=True, vmem_limit_bytes=60 << 20
        ),
    )(region_of, pairs, basis, activity)


def order_kernel(lags_hbm, raw_ref, out_ref, lags_ref, place, given, result, lags_sem, in_sem, sem):
    nlag, side = lags_ref.shape[0], raw_ref.shape[1]
    width = side // nlag
    parts = sem.shape[0]
    size = raw_ref.shape[0] // parts

    def load(n):
        rows = pl.ds(n * size, size)
        return pltpu.make_async_copy(raw_ref.at[rows], given.at[rows], in_sem.at[n])

    def store(n):
        rows = pl.ds(n * size, size)
        return pltpu.make_async_copy(result.at[rows], out_ref.at[rows], sem.at[n])

    lags_load = pltpu.make_async_copy(lags_hbm, lags_ref, lags_sem)
    lags_load.start()
    for n in range(parts):
        load(n).start()
    lags_load.wait()
    shift = lax.broadcasted_iota(jnp.int32, (side, width), 0) - lax.broadcasted_iota(jnp.int32, (side, width), 1)
    for m in range(nlag):
        place[:, m * width:(m + 1) * width] = jnp.where(shift == lags_ref[m] * width, 1.0, 0.0).astype(jnp.bfloat16)
    for n in range(parts):
        load(n).wait()
        rows = slice(n * size, (n + 1) * size)
        result[rows] = jnp.dot(given[rows], place[...], preferred_element_type=jnp.float32).astype(jnp.bfloat16)
        store(n).start()
    for n in range(parts):
        store(n).wait()


def ordered(raw, lags):
    total, side = raw.shape
    parts = 2
    return pl.pallas_call(
        order_kernel,
        in_specs=[pl.BlockSpec(memory_space=pl.ANY)] * 2,
        out_specs=pl.BlockSpec(memory_space=pl.ANY),
        out_shape=jax.ShapeDtypeStruct((total, side), jnp.bfloat16),
        scratch_shapes=[
            pltpu.SMEM(lags.shape, jnp.int32),
            pltpu.VMEM((side, side), jnp.bfloat16),
            pltpu.VMEM((total, side), jnp.bfloat16),
            pltpu.VMEM((total, side), jnp.bfloat16),
            pltpu.SemaphoreType.DMA,
            pltpu.SemaphoreType.DMA((parts,)),
            pltpu.SemaphoreType.DMA((parts,)),
        ],
    )(lags, raw)


def local(shape, activity, basis, region_of, pairs, lags):
    raw = raw_covariances(shape, lags.shape[0], region_of, pairs.T, basis.T, activity)
    return ordered(raw, lags).reshape(pairs.shape[0], basis.shape[1], -1)


def solution(mesh):
    shape = (mesh.shape["row"], mesh.shape["col"], mesh.shape["reg"])
    return jax.shard_map(
        functools.partial(local, shape),
        mesh=mesh,
        in_specs=(
            P(("row", "col", "reg"), None),
            P(("row", "col", "reg"), None),
            P(("row", "col", "reg")),
            P(("row", "col", "reg"), None),
            P(),
        ),
        out_specs=P(("row", "col", "reg"), None, None),
        check_vma=False,
    )
```
